32 devices in a mesh: batch: 2 (over x), strip: 8 (over z, y), plate: 2 (over core).
Axes of the slice: x: 2, y: 2, z: 4, core: 2. Of those that a mesh axis runs over, the one named last changes fastest.
Arguments:
- fields: bfloat16 [32, 1088, 5, 1080], P(('batch', 'strip', 'plate')), parts along dimension 0, may hold values from 0.05 to 80, as said below
- flat_gain: bfloat16 [1088, 5, 1080], P('strip'), may hold values from 0.5 to 1.5
Outputs:
- corrected: bfloat16 [32, 1088, 5, 1080], P(('batch', 'strip', 'plate')), parts along dimension 0
- illumination: float32 [1088, 10, 1080], P('strip', 'batch'), parts along dimension 1
- mean_field: float32 [1088, 10, 1080], P('strip', 'batch'), parts along dimension 1
The draws below stay inside these ranges and needn't reach their ends.
There are 2 independent parts, one for each index of `batch`. The reference program is written for one: setup_inputs(seed, part) draws one part's arguments, and reference() takes and returns one part's arrays. A program takes and returns all parts, laid end to end along the dimension named above; an argument that names none is the same for every part. Nothing has to cross between parts.
Inputs may be any that keep to these rules, and one draw needn't show every extreme that they name: `fields`: positive intensities.
All inputs are finite; a program needn't handle non-finite values.
Results may differ from the reference program's by a relative error of at most 0.0004.
The reference program's roundings to bfloat16 on the way (of `illum_round`) count: a program that leaves them out, or rounds other values in their place, can miss the bound.
Values may be sent and summed in bfloat16 or wider, within the bound.
A program may use at most 192 MiB of HBM per device.

```python
import math
import jax
import jax.numpy as jnp
from jax import lax

C = 5
H = 1088
W = 1080
SIGMA = 16
RADIUS = 48
FIELDS = 16


def draw_fields(key, part):
    key_bright, key_texture = jax.random.split(key, 2)
    rows = jnp.arange(H, dtype=jnp.float32) / H - 0.5
    cols = jnp.arange(W, dtype=jnp.float32) / W - 0.5
    vignette = 0.4 + jnp.exp(-(rows[:, None, None] ** 2 + cols[None, None, :] ** 2) / 0.18)
    bright = jnp.exp(jax.random.uniform(key_bright, (FIELDS, 1, C, 1), jnp.float32, 0.0, math.log(10.0)))
    texture = jax.random.uniform(key_texture, (FIELDS, H, C, W), jnp.float32, 0.3, 3.0)
    return (bright * vignette[None] * texture).astype(jnp.bfloat16)


def setup_inputs(seed: int = 0, part: int = 0) -> dict:
    key_of = jax.random.split(jax.random.key(seed), 3)
    part_splits = jax.random.split(jax.random.fold_in(key_of[2], part), 3)
    return {
        "fields": draw_fields(jax.random.fold_in(jax.random.fold_in(key_of[2], part), 71), part),
        "flat_gain": jnp.clip(1.0 + 0.1 * jax.random.normal(key_of[1], (H, C, W), jnp.float32), 0.5, 1.5).astype(jnp.bfloat16),
    }


def kernel_table(length):
    index = jnp.arange(length, dtype=jnp.float32)
    offset = index[:, None] - index[None, :]
    weights = jnp.where(jnp.abs(offset) <= RADIUS, jnp.exp(-offset * offset / (2.0 * SIGMA * SIGMA)), 0.0)
    return weights / jnp.sum(weights, axis=1, keepdims=True)


def reference(fields, flat_gain):
    def accumulate(carry, field):
        return carry + field.astype(jnp.float32), None

    total, unused = lax.scan(accumulate, jnp.zeros((H, C, W), jnp.float32), fields)
    mean_field = total / FIELDS
    smooth_cols = jnp.einsum("hcv,wv->hcw", mean_field, kernel_table(W), precision=lax.Precision.HIGHEST)
    illumination = jnp.einsum("hu,ucw->hcw", kernel_table(H), smooth_cols, precision=lax.Precision.HIGHEST)
    illum_round = (illumination * flat_gain.astype(jnp.float32)).astype(jnp.bfloat16).astype(jnp.float32)

    def divide(field):
        return (field.astype(jnp.float32) / illum_round).astype(jnp.bfloat16)

    corrected = lax.map(divide, fields)
    return corrected, illumination, mean_field
```

```python
import functools
import jax
import jax.numpy as jnp
from jax import lax
from jax.experimental import pallas as pl
from jax.experimental.pallas import tpu as pltpu
from jax.sharding import PartitionSpec as P

SIGMA = 16
RADIUS = 48
ROWS = 8
MESH = pl.DeviceIdType.MESH
LINK = jnp.bfloat16


def coded(mean):
    for _ in range(4):
        mean = mean * mean
    return mean.astype(LINK)


def decoded(code):
    code = code.astype(jnp.float32)
    for _ in range(4):
        code = lax.rsqrt(code)
    return code


def padded_2(array, sides, width):
    for axis, dim in sides:
        count, length = (lax.axis_size(axis), array.shape[dim])
        up = [(i, (i + 1) % count) for i in range(count - 1)]
        down = [(j, i) for i, j in up]
        last = lax.slice_in_dim(array, length - width, length, axis=dim)
        first = lax.slice_in_dim(array, 0, width, axis=dim)
        before = lax.ppermute(last, axis, up)
        after = lax.ppermute(first, axis, down)
        array = jnp.concatenate([before, array, after], axis=dim)
    return array


def gauss_weights(out_index, in_index, length):
    offset = out_index[:, None] - in_index[None, :]
    inside = (jnp.abs(offset) <= RADIUS) & (in_index[None, :] >= 0.0) & (in_index[None, :] < length)
    weights = jnp.where(inside, jnp.exp(-offset * offset / (2.0 * SIGMA * SIGMA)), 0.0)
    return weights / jnp.sum(weights, axis=1, keepdims=True)


def where_am_i():
    strip, plate = lax.axis_index("strip"), lax.axis_index("plate")
    return strip, plate, lax.rem(strip, 2), lax.div(strip, 2)


def at(strip, plate):
    return {"strip": strip, "plate": plate}


def greet(nz, strip, plate, y, z):
    barrier = pltpu.get_barrier_semaphore()
    partners = [at(strip, 1 - plate), at(z * 2 + 1 - y, plate)]
    partners += [at(lax.rem(z + d, nz) * 2 + y, plate) for d in range(1, nz)]
    for partner in partners:
        pl.semaphore_signal(barrier, inc=1, device_id=partner, device_id_type=MESH)
    pl.semaphore_wait(barrier, len(partners))


def reduce_kernel(x_ref, out_ref, mine, sib, pair, ybuf, zsend, zbuf, total,
                  load_sem, sib_send, sib_recv, y_send, y_recv, z_send, z_recv, t_send, t_recv, o_sem):
    channels, nz, _, rows, _ = x_ref.shape
    strip, plate, y, z = where_am_i()
    active = y == plate
    sibling = at(strip, 1 - plate)
    greet(nz, strip, plate, y, z)

    def load(c):
        return pltpu.make_async_copy(x_ref.at[c, :, plate], mine.at[c], load_sem.at[c])

    def to_sibling(c):
        return pltpu.make_async_remote_copy(
            x_ref.at[c, :, 1 - plate], sib.at[c], sib_send.at[c], sib_recv.at[c],
            device_id=sibling, device_id_type=MESH)

    def across(c):
        return pltpu.make_async_remote_copy(
            pair.at[c], ybuf.at[c], y_send.at[c], y_recv.at[c],
            device_id=at(z * 2 + 1 - y, plate), device_id_type=MESH)

    def along(c, d):
        return pltpu.make_async_remote_copy(
            zsend.at[c, d], zbuf.at[c, d], z_send.at[c, d], z_recv.at[c, d],
            device_id=at(lax.rem(z + d, nz) * 2 + y, plate), device_id_type=MESH)

    def share(c):
        return pltpu.make_async_remote_copy(
            total.at[c], total.at[c], t_send.at[c], t_recv.at[c],
            device_id=sibling, device_id_type=MESH)

    def store(c):
        return pltpu.make_async_copy(total.at[c], out_ref.at[c], o_sem.at[c])

    @pl.loop(0, channels)
    def _(c):
        load(c).start()
        to_sibling(c).start()

    @pl.loop(0, channels)
    def _(c):
        load(c).wait()
        to_sibling(c).wait_recv()

        @pl.when(jnp.logical_not(active))
        def _():
            @pl.loop(0, nz)
            def _(k):
                for r in range(0, rows, ROWS):
                    at_r = pl.ds(r, ROWS)
                    value = mine[c, k, at_r, :].astype(jnp.float32) + sib[c, k, at_r, :].astype(jnp.float32)
                    pair[c, k, at_r, :] = coded(value * 0.5)

            across(c).start()

    @pl.when(active)
    def _():
        @pl.loop(0, channels)
        def _(c):
            across(c).wait_recv()

            def summed(k, r):
                at_r = pl.ds(r, ROWS)
                value = mine[c, k, at_r, :].astype(jnp.float32) + sib[c, k, at_r, :].astype(jnp.float32)
                return value + 2.0 * decoded(ybuf[c, k, at_r, :])

            @pl.loop(1, nz)
            def _(d):
                k = lax.rem(z + d, nz)
                for r in range(0, rows, ROWS):
                    zsend[c, d, pl.ds(r, ROWS), :] = coded(summed(k, r) * 0.25)
                along(c, d).start()

            for r in range(0, rows, ROWS):
                total[c, pl.ds(r, ROWS), :] = summed(z, r)

        @pl.loop(0, channels)
        def _(c):
            @pl.loop(1, nz)
            def _(d):
                along(c, d).wait_recv()

            for r in range(0, rows, ROWS):
                at_r = pl.ds(r, ROWS)
                value = total[c, at_r, :]
                for d in range(1, nz):
                    value = value + 4.0 * decoded(zbuf[c, d, at_r, :])
                total[c, at_r, :] = value
            share(c).start()
            store(c).start()

        @pl.loop(0, channels)
        def _(c):
            share(c).wait_send()

            @pl.loop(1, nz)
            def _(d):
                along(c, d).wait_send()

    @pl.when(jnp.logical_not(active))
    def _():
        @pl.loop(0, channels)
        def _(c):
            share(c).wait_recv()
            store(c).start()
            across(c).wait_send()

    @pl.loop(0, channels)
    def _(c):
        to_sibling(c).wait_send()
        store(c).wait()


def strip_totals(x):
    channels, nz, _, rows, width = x.shape
    part = (channels, nz, rows, width)
    dma = pltpu.SemaphoreType.DMA
    return pl.pallas_call(
        reduce_kernel,
        out_shape=jax.ShapeDtypeStruct((channels, rows, width), jnp.float32),
        in_specs=[pl.BlockSpec(memory_space=pl.ANY)],
        out_specs=pl.BlockSpec(memory_space=pl.ANY),
        scratch_shapes=[
            pltpu.VMEM(part, x.dtype), pltpu.VMEM(part, x.dtype),
            pltpu.VMEM(part, LINK), pltpu.VMEM(part, LINK),
            pltpu.VMEM(part, LINK), pltpu.VMEM(part, LINK),
            pltpu.VMEM((channels, rows, width), jnp.float32),
            dma((channels,)), dma((channels,)), dma((channels,)), dma((channels,)), dma((channels,)),
            dma((channels, nz)), dma((channels, nz)), dma((channels,)), dma((channels,)), dma((channels,)),
        ],
        compiler_params=pltpu.CompilerParams(
            collective_id=0, has_side_effects=True, vmem_limit_bytes=56 * 2**20),
        name="strip_totals",
    )(x)


def gather_kernel(own_ref, out_ref, own_sem, recv_sem, send_sem):
    channels, nz = out_ref.shape[:2]
    strip, plate, y, z = where_am_i()
    active = y == plate
    greet(nz, strip, plate, y, z)
    sibling, across = at(strip, 1 - plate), at(z * 2 + 1 - y, plate)
    above, below = at((z + 1) * 2 + y, plate), at((z - 1) * 2 + y, plate)

    def own(c):
        return pltpu.make_async_copy(own_ref.at[c], out_ref.at[c, z, y], own_sem.at[c])

    def send(c, k, column, kind, target, src=None):
        slot = out_ref.at[c, k, column]
        return pltpu.make_async_remote_copy(
            slot if src is None else src, slot, send_sem.at[c, k, kind], recv_sem.at[c, k, column],
            device_id=target, device_id_type=MESH)

    def sides(d, up, down):
        pl.when(z - d >= 0)(lambda: up(z - d))
        pl.when(z + d < nz)(lambda: down(z + d))

    @pl.when(active)
    def _():
        @pl.loop(0, channels)
        def _(c):
            own(c).start()
            pl.when(z + 1 < nz)(lambda: send(c, z, y, 2, above, own_ref.at[c]).start())
            pl.when(z >= 1)(lambda: send(c, z, y, 3, below, own_ref.at[c]).start())
            send(c, z, y, 1, across, own_ref.at[c]).start()
            send(c, z, y, 0, sibling, own_ref.at[c]).start()

        @pl.loop(1, nz)
        def _(d):
            @pl.loop(0, channels)
            def _(c):
                def up(k):
                    send(c, k, y, 2, above).wait_recv()
                    pl.when(z + 1 < nz)(lambda: send(c, k, y, 2, above).start())
                    send(c, k, y, 1, across).start()
                    send(c, k, y, 0, sibling).start()

                def down(k):
                    send(c, k, y, 3, below).wait_recv()
                    pl.when(z >= 1)(lambda: send(c, k, y, 3, below).start())
                    send(c, k, y, 1, across).start()
                    send(c, k, y, 0, sibling).start()

                sides(d, up, down)

        @pl.loop(0, channels)
        def _(c):
            own(c).wait()

            @pl.loop(0, nz)
            def _(k):
                send(c, k, 1 - y, 0, sibling).wait_recv()
                send(c, k, y, 0, sibling).wait_send()
                send(c, k, y, 1, across).wait_send()
                pl.when((k <= z) & (z + 1 < nz))(lambda: send(c, k, y, 2, above).wait_send())
                pl.when((k >= z) & (z >= 1))(lambda: send(c, k, y, 3, below).wait_send())

    @pl.when(jnp.logical_not(active))
    def _():
        @pl.loop(0, nz)
        def _(d):
            @pl.loop(0, channels)
            def _(c):
                def relay(k):
                    send(c, k, 1 - y, 0, sibling).wait_recv()
                    send(c, k, 1 - y, 0, sibling).start()

                pl.when(z - d >= 0)(lambda: relay(z - d))
                pl.when((z + d < nz) & (d > 0))(lambda: relay(z + d))

        @pl.loop(0, channels)
        def _(c):
            @pl.loop(0, nz)
            def _(k):
                send(c, k, y, 0, sibling).wait_recv()
                send(c, k, 1 - y, 0, sibling).wait_send()


def gathered(own, nz):
    channels, rows, width = own.shape
    dma = pltpu.SemaphoreType.DMA
    return pl.pallas_call(
        gather_kernel,
        out_shape=jax.ShapeDtypeStruct((channels, nz, 2, rows, width), own.dtype),
        in_specs=[pl.BlockSpec(memory_space=pl.ANY)],
        out_specs=pl.BlockSpec(memory_space=pl.ANY),
        scratch_shapes=[dma((channels,)), dma((channels, nz, 2)), dma((channels, nz, 4))],
        compiler_params=pltpu.CompilerParams(collective_id=1, has_side_effects=True),
        name="gathered",
    )(own)


def on_grid(fields, flat_gain):
    _, height, channels, width = fields.shape
    strips = lax.axis_size("strip")
    nz = strips // 2
    strip_rows = height // strips
    both = ("strip", "plate")
    x = jnp.transpose(fields[0], (1, 0, 2))
    total = strip_totals(x.reshape(channels, nz, 2, strip_rows, width))
    mean_field = total / (strips * 2)
    col_index = jnp.arange(width, dtype=jnp.float32)
    col_kernel = gauss_weights(col_index, col_index, float(width))
    smooth_cols = jnp.einsum("chv,wv->chw", mean_field, col_kernel, precision=lax.Precision.HIGHEST)
    up = [(i * 2 + i % 2, (i + 1) * 2 + (i + 1) % 2) for i in range(strips - 1)]
    down = [(j, i) for i, j in up]
    before = lax.ppermute(smooth_cols[:, strip_rows - RADIUS:], both, up)
    after = lax.ppermute(smooth_cols[:, :RADIUS], both, down)
    padded = jnp.concatenate([before, smooth_cols, after], axis=1)
    strip = lax.axis_index("strip")
    first_row = (strip * strip_rows).astype(jnp.float32)
    out_index = first_row + jnp.arange(strip_rows, dtype=jnp.float32)
    in_index = first_row - RADIUS + jnp.arange(strip_rows + 2 * RADIUS, dtype=jnp.float32)
    row_kernel = gauss_weights(out_index, in_index, float(height))
    illumination = jnp.einsum("hu,cuw->chw", row_kernel, padded, precision=lax.Precision.HIGHEST)
    gain = jnp.transpose(flat_gain, (1, 0, 2)).astype(jnp.float32)
    illum_round = (illumination * gain).astype(jnp.bfloat16)
    everywhere = gathered(illum_round, nz).reshape(channels, height, width)
    twins = [(i * 2 + i % 2, i * 2 + 1 - i % 2) for i in range(strips)]
    twin = lax.ppermute(illumination, both, twins)
    illumination = jnp.where(lax.rem(strip, 2) == lax.axis_index("plate"), illumination, twin)
    corrected = (x.astype(jnp.float32) / everywhere.astype(jnp.float32)).astype(jnp.bfloat16)
    back = lambda a: jnp.transpose(a, (1, 0, 2))
    return (back(corrected)[None], back(illumination), back(mean_field))


def on_device(fields, flat_gain):
    num_fields, height, channels, width = fields.shape
    strips = lax.axis_size("strip")
    plates = lax.axis_size("plate")
    strip_rows = height // strips
    count = num_fields * strips * plates
    block = fields
    partial_sum = lax.psum_scatter(
        jnp.sum(block, axis=0, dtype=jnp.float32), "strip", scatter_dimension=0, tiled=True
    )
    total = lax.psum(partial_sum, "plate")
    mean_field = total / count
    col_index = jnp.arange(width, dtype=jnp.float32)
    col_kernel = gauss_weights(col_index, col_index, float(width))
    smooth_cols = jnp.einsum("hcv,wv->hcw", mean_field, col_kernel, precision=lax.Precision.HIGHEST)
    padded = padded_2(smooth_cols, (("strip", 0),), RADIUS)
    first_row = (lax.axis_index("strip") * strip_rows).astype(jnp.float32)
    out_index = first_row + jnp.arange(strip_rows, dtype=jnp.float32)
    in_index = first_row - RADIUS + jnp.arange(strip_rows + 2 * RADIUS, dtype=jnp.float32)
    row_kernel = gauss_weights(out_index, in_index, float(height))
    illumination = jnp.einsum("hu,ucw->hcw", row_kernel, padded, precision=lax.Precision.HIGHEST)
    illum_round = (illumination * flat_gain.astype(jnp.float32)).astype(jnp.bfloat16)
    block = fields
    corrected = (
        block.astype(jnp.float32)
        / lax.all_gather(illum_round, "strip", axis=0, tiled=True).astype(jnp.float32)[None]
    ).astype(jnp.bfloat16)
    return (corrected, illumination, mean_field)


def solution(mesh):
    grid = mesh.shape["strip"] == 8 and mesh.shape["plate"] == 2
    return jax.shard_map(
        on_grid if grid else on_device,
        mesh=mesh,
        in_specs=(P(("batch", "strip", "plate"), None, None, None), P("strip", None, None)),
        out_specs=(
            P(("batch", "strip", "plate"), None, None, None),
            P("strip", "batch", None),
            P("strip", "batch", None),
        ),
        check_vma=False,
    )
```

```python
import jax
import jax.numpy as jnp
from jax import lax
from jax.experimental import pallas as pl
from jax.experimental.pallas import tpu as pltpu
from jax.sharding import PartitionSpec as P

SIGMA = 16
RADIUS = 48
ROWS = 8
COLUMNS = lax.Precision.HIGH
MESH = pl.DeviceIdType.MESH
LINK = jnp.bfloat16


def coded(mean):
    for _ in range(4):
        mean = mean * mean
    return mean.astype(LINK)


def decoded(code):
    code = code.astype(jnp.float32)
    for _ in range(4):
        code = lax.rsqrt(code)
    return code


def padded_2(array, sides, width):
    for axis, dim in sides:
        count, length = (lax.axis_size(axis), array.shape[dim])
        up = [(i, (i + 1) % count) for i in range(count - 1)]
        down = [(j, i) for i, j in up]
        last = lax.slice_in_dim(array, length - width, length, axis=dim)
        first = lax.slice_in_dim(array, 0, width, axis=dim)
        before = lax.ppermute(last, axis, up)
        after = lax.ppermute(first, axis, down)
        array = jnp.concatenate([before, array, after], axis=dim)
    return array


def gauss_weights(out_index, in_index, length):
    offset = out_index[:, None] - in_index[None, :]
    inside = (jnp.abs(offset) <= RADIUS) & (in_index[None, :] >= 0.0) & (in_index[None, :] < length)
    weights = jnp.where(inside, jnp.exp(-offset * offset / (2.0 * SIGMA * SIGMA)), 0.0)
    return weights / jnp.sum(weights, axis=1, keepdims=True)


def where_am_i():
    strip, plate = lax.axis_index("strip"), lax.axis_index("plate")
    return strip, plate, lax.rem(strip, 2), lax.div(strip, 2)


def at(strip, plate):
    return {"strip": strip, "plate": plate}


def greet(nz, strip, plate, y, z, halo=False):
    barrier = pltpu.get_barrier_semaphore()
    partners = [at(strip, 1 - plate), at(z * 2 + 1 - y, plate)]
    if halo:
        partners += [at(lax.rem(strip + d, nz * 2), 1 - plate) for d in (1, nz * 2 - 1)]
    partners += [at(lax.rem(z + d, nz) * 2 + y, plate) for d in range(1, nz)]
    for partner in partners:
        pl.semaphore_signal(barrier, inc=1, device_id=partner, device_id_type=MESH)
    pl.semaphore_wait(barrier, len(partners))


def reduce_kernel(x_ref, out_ref, mine, sib, pair, ybuf, zsend, zbuf, total,
                  load_sem, sib_send, sib_recv, y_send, y_recv, z_send, z_recv, t_send, t_recv, h_send, h_recv, o_sem):
    channels, nz, _, rows, width = x_ref.shape
    strip, plate, y, z = where_am_i()
    active = y == plate
    sibling = at(strip, 1 - plate)
    strips = nz * 2
    inner = pl.ds(RADIUS, rows)
    has_before, has_after = strip >= 1, strip + 1 < strips
    greet(nz, strip, plate, y, z, halo=True)

    def load(c):
        return pltpu.make_async_copy(x_ref.at[c, :, plate], mine.at[c], load_sem.at[c])

    def to_sibling(c):
        return pltpu.make_async_remote_copy(
            x_ref.at[c, :, 1 - plate], sib.at[c], sib_send.at[c], sib_recv.at[c],
            device_id=sibling, device_id_type=MESH)

    def across(c):
        return pltpu.make_async_remote_copy(
            pair.at[c], ybuf.at[c], y_send.at[c], y_recv.at[c],
            device_id=at(z * 2 + 1 - y, plate), device_id_type=MESH)

    def along(c, d):
        return pltpu.make_async_remote_copy(
            zsend.at[c, d], zbuf.at[c, d], z_send.at[c, d], z_recv.at[c, d],
            device_id=at(lax.rem(z + d, nz) * 2 + y, plate), device_id_type=MESH)

    def halo_up(c):
        return pltpu.make_async_remote_copy(
            total.at[c, pl.ds(rows, RADIUS)], total.at[c, pl.ds(0, RADIUS)], h_send.at[c, 0], h_recv.at[c, 0],
            device_id=at(lax.rem(strip + 1, strips), 1 - plate), device_id_type=MESH)

    def halo_down(c):
        return pltpu.make_async_remote_copy(
            total.at[c, inner].at[pl.ds(0, RADIUS)], total.at[c, pl.ds(RADIUS + rows, RADIUS)],
            h_send.at[c, 1], h_recv.at[c, 1],
            device_id=at(lax.rem(strip + strips - 1, strips), 1 - plate), device_id_type=MESH)

    def share(c):
        return pltpu.make_async_remote_copy(
            total.at[c], total.at[c], t_send.at[c], t_recv.at[c],
            device_id=sibling, device_id_type=MESH)

    def store(c):
        return pltpu.make_async_copy(total.at[c], out_ref.at[c], o_sem.at[c])

    @pl.loop(0, channels)
    def _(c):
        load(c).start()
        to_sibling(c).start()

    @pl.loop(0, channels)
    def _(c):
        load(c).wait()
        to_sibling(c).wait_recv()

        @pl.when(jnp.logical_not(active))
        def _():
            @pl.loop(0, nz)
            def _(k):
                for r in range(0, rows, ROWS):
                    at_r = pl.ds(r, ROWS)
                    value = mine[c, k, at_r, :].astype(jnp.float32) + sib[c, k, at_r, :].astype(jnp.float32)
                    pair[c, k, at_r, :] = coded(value * 0.5)

            across(c).start()

    @pl.when(active)
    def _():
        @pl.loop(0, channels)
        def _(c):
            across(c).wait_recv()

            def summed(k, r):
                at_r = pl.ds(r, ROWS)
                value = mine[c, k, at_r, :].astype(jnp.float32) + sib[c, k, at_r, :].astype(jnp.float32)
                return value + 2.0 * decoded(ybuf[c, k, at_r, :])

            @pl.loop(1, nz)
            def _(d):
                k = lax.rem(z + d, nz)
                for r in range(0, rows, ROWS):
                    zsend[c, d, pl.ds(r, ROWS), :] = coded(summed(k, r) * 0.25)
                along(c, d).start()

            for r in range(0, rows, ROWS):
                total[c, pl.ds(RADIUS + r, ROWS), :] = summed(z, r)

        @pl.loop(0, channels)
        def _(c):
            @pl.loop(1, nz)
            def _(d):
                along(c, d).wait_recv()

            for r in range(0, rows, ROWS):
                at_r = pl.ds(r, ROWS)
                value = total[c, pl.ds(RADIUS + r, ROWS), :]
                for d in range(1, nz):
                    value = value + 4.0 * decoded(zbuf[c, d, at_r, :])
                total[c, pl.ds(RADIUS + r, ROWS), :] = value
            pl.when(has_after)(lambda: halo_up(c).start())
            pl.when(has_before)(lambda: halo_down(c).start())

        outside = jnp.zeros((RADIUS, width), jnp.float32)

        @pl.loop(0, channels)
        def _(c):
            @pl.when(has_before)
            def _():
                halo_up(c).wait_recv()

            @pl.when(jnp.logical_not(has_before))
            def _():
                total[c, pl.ds(0, RADIUS), :] = outside

            @pl.when(has_after)
            def _():
                halo_down(c).wait_recv()

            @pl.when(jnp.logical_not(has_after))
            def _():
                total[c, pl.ds(RADIUS + rows, RADIUS), :] = outside

            share(c).start()
            store(c).start()

        @pl.loop(0, channels)
        def _(c):
            share(c).wait_send()
            pl.when(has_after)(lambda: halo_up(c).wait_send())
            pl.when(has_before)(lambda: halo_down(c).wait_send())

            @pl.loop(1, nz)
            def _(d):
                along(c, d).wait_send()

    @pl.when(jnp.logical_not(active))
    def _():
        @pl.loop(0, channels)
        def _(c):
            share(c).wait_recv()
            store(c).start()
            across(c).wait_send()

    @pl.loop(0, channels)
    def _(c):
        to_sibling(c).wait_send()
        store(c).wait()


def strip_totals(x):
    channels, nz, _, rows, width = x.shape
    part = (channels, nz, rows, width)
    dma = pltpu.SemaphoreType.DMA
    return pl.pallas_call(
        reduce_kernel,
        out_shape=jax.ShapeDtypeStruct((channels, rows + 2 * RADIUS, width), jnp.float32),
        in_specs=[pl.BlockSpec(memory_space=pl.ANY)],
        out_specs=pl.BlockSpec(memory_space=pl.ANY),
        scratch_shapes=[
            pltpu.VMEM(part, x.dtype), pltpu.VMEM(part, x.dtype),
            pltpu.VMEM(part, LINK), pltpu.VMEM(part, LINK),
            pltpu.VMEM(part, LINK), pltpu.VMEM(part, LINK),
            pltpu.VMEM((channels, rows + 2 * RADIUS, width), jnp.float32),
            dma((channels,)), dma((channels,)), dma((channels,)), dma((channels,)), dma((channels,)),
            dma((channels, nz)), dma((channels, nz)), dma((channels,)), dma((channels,)),
            dma((channels, 2)), dma((channels, 2)), dma((channels,)),
        ],
        compiler_params=pltpu.CompilerParams(
            collective_id=0, has_side_effects=True, vmem_limit_bytes=56 * 2**20),
        name="strip_totals",
    )(x)


def gather_kernel(own_ref, out_ref, own_sem, recv_sem, send_sem):
    channels, nz = out_ref.shape[:2]
    strip, plate, y, z = where_am_i()
    active = y == plate
    greet(nz, strip, plate, y, z)
    sibling, across = at(strip, 1 - plate), at(z * 2 + 1 - y, plate)
    above, below = at((z + 1) * 2 + y, plate), at((z - 1) * 2 + y, plate)

    def own(c):
        return pltpu.make_async_copy(own_ref.at[c], out_ref.at[c, z, y], own_sem.at[c])

    def send(c, k, column, kind, target, src=None):
        slot = out_ref.at[c, k, column]
        return pltpu.make_async_remote_copy(
            slot if src is None else src, slot, send_sem.at[c, k, kind], recv_sem.at[c, k, column],
            device_id=target, device_id_type=MESH)

    def sides(d, up, down):
        pl.when(z - d >= 0)(lambda: up(z - d))
        pl.when(z + d < nz)(lambda: down(z + d))

    @pl.when(active)
    def _():
        @pl.loop(0, channels)
        def _(c):
            own(c).start()
            pl.when(z + 1 < nz)(lambda: send(c, z, y, 2, above, own_ref.at[c]).start())
            pl.when(z >= 1)(lambda: send(c, z, y, 3, below, own_ref.at[c]).start())
            send(c, z, y, 1, across, own_ref.at[c]).start()
            send(c, z, y, 0, sibling, own_ref.at[c]).start()

        @pl.loop(1, nz)
        def _(d):
            @pl.loop(0, channels)
            def _(c):
                def up(k):
                    send(c, k, y, 2, above).wait_recv()
                    pl.when(z + 1 < nz)(lambda: send(c, k, y, 2, above).start())
                    send(c, k, y, 1, across).start()
                    send(c, k, y, 0, sibling).start()

                def down(k):
                    send(c, k, y, 3, below).wait_recv()
                    pl.when(z >= 1)(lambda: send(c, k, y, 3, below).start())
                    send(c, k, y, 1, across).start()
                    send(c, k, y, 0, sibling).start()

                sides(d, up, down)

        @pl.loop(0, channels)
        def _(c):
            own(c).wait()

            @pl.loop(0, nz)
            def _(k):
                send(c, k, 1 - y, 0, sibling).wait_recv()
                send(c, k, y, 0, sibling).wait_send()
                send(c, k, y, 1, across).wait_send()
                pl.when((k <= z) & (z + 1 < nz))(lambda: send(c, k, y, 2, above).wait_send())
                pl.when((k >= z) & (z >= 1))(lambda: send(c, k, y, 3, below).wait_send())

    @pl.when(jnp.logical_not(active))
    def _():
        @pl.loop(0, nz)
        def _(d):
            @pl.loop(0, channels)
            def _(c):
                def relay(k):
                    send(c, k, 1 - y, 0, sibling).wait_recv()
                    send(c, k, 1 - y, 0, sibling).start()

                pl.when(z - d >= 0)(lambda: relay(z - d))
                pl.when((z + d < nz) & (d > 0))(lambda: relay(z + d))

        @pl.loop(0, channels)
        def _(c):
            @pl.loop(0, nz)
            def _(k):
                send(c, k, y, 0, sibling).wait_recv()
                send(c, k, 1 - y, 0, sibling).wait_send()


def gathered(own, nz):
    channels, rows, width = own.shape
    dma = pltpu.SemaphoreType.DMA
    return pl.pallas_call(
        gather_kernel,
        out_shape=jax.ShapeDtypeStruct((channels, nz, 2, rows, width), own.dtype),
        in_specs=[pl.BlockSpec(memory_space=pl.ANY)],
        out_specs=pl.BlockSpec(memory_space=pl.ANY),
        scratch_shapes=[dma((channels,)), dma((channels, nz, 2)), dma((channels, nz, 4))],
        compiler_params=pltpu.CompilerParams(collective_id=1, has_side_effects=True),
        name="gathered",
    )(own)


def divide_kernel(field_ref, illum_ref, out_ref):
    illum = jnp.transpose(illum_ref[0]).astype(jnp.float32)
    out_ref[0] = (field_ref[0].astype(jnp.float32) / illum).astype(out_ref.dtype)


def divided(field, illum):
    channels, width, height = field.shape
    wide = 256
    upright = pl.BlockSpec((1, wide, height), lambda c, w: (c, w, 0))
    return pl.pallas_call(
        divide_kernel,
        grid=(channels, pl.cdiv(width, wide)),
        out_shape=jax.ShapeDtypeStruct(field.shape, field.dtype),
        in_specs=[upright, pl.BlockSpec((1, height, wide), lambda c, w: (c, 0, w))],
        out_specs=upright,
        compiler_params=pltpu.CompilerParams(vmem_limit_bytes=40 * 2**20),
        name="divided",
    )(field, illum)


def on_grid(fields, flat_gain):
    _, height, channels, width = fields.shape
    strips = lax.axis_size("strip")
    nz = strips // 2
    strip_rows = height // strips
    x = jnp.transpose(fields[0], (1, 0, 2))
    padded = strip_totals(x.reshape(channels, nz, 2, strip_rows, width)) / (strips * 2)
    mean_field = padded[:, RADIUS:RADIUS + strip_rows]
    first_row = (lax.axis_index("strip") * strip_rows).astype(jnp.float32)
    out_index = first_row + jnp.arange(strip_rows, dtype=jnp.float32)
    in_index = first_row - RADIUS + jnp.arange(strip_rows + 2 * RADIUS, dtype=jnp.float32)
    row_kernel = gauss_weights(out_index, in_index, float(height))
    smooth_rows = jnp.einsum("hu,cuw->chw", row_kernel, padded, precision=lax.Precision.HIGHEST)
    col_index = jnp.arange(width, dtype=jnp.float32)
    col_kernel = gauss_weights(col_index, col_index, float(width))
    illumination = jnp.einsum("chv,wv->chw", smooth_rows, col_kernel, precision=COLUMNS)
    gain = jnp.transpose(flat_gain, (1, 0, 2)).astype(jnp.float32)
    illum_round = (illumination * gain).astype(jnp.bfloat16)
    everywhere = gathered(illum_round, nz).reshape(channels, height, width)
    corrected = divided(jnp.transpose(fields[0], (1, 2, 0)), everywhere)
    back = lambda a: jnp.transpose(a, (1, 0, 2))
    return (jnp.transpose(corrected, (2, 0, 1))[None], back(illumination), back(mean_field))


def on_device(fields, flat_gain):
    num_fields, height, channels, width = fields.shape
    strips = lax.axis_size("strip")
    plates = lax.axis_size("plate")
    strip_rows = height // strips
    count = num_fields * strips * plates
    block = fields
    partial_sum = lax.psum_scatter(
        jnp.sum(block, axis=0, dtype=jnp.float32), "strip", scatter_dimension=0, tiled=True
    )
    total = lax.psum(partial_sum, "plate")
    mean_field = total / count
    col_index = jnp.arange(width, dtype=jnp.float32)
    col_kernel = gauss_weights(col_index, col_index, float(width))
    smooth_cols = jnp.einsum("hcv,wv->hcw", mean_field, col_kernel, precision=lax.Precision.HIGHEST)
    padded = padded_2(smooth_cols, (("strip", 0),), RADIUS)
    first_row = (lax.axis_index("strip") * strip_rows).astype(jnp.float32)
    out_index = first_row + jnp.arange(strip_rows, dtype=jnp.float32)
    in_index = first_row - RADIUS + jnp.arange(strip_rows + 2 * RADIUS, dtype=jnp.float32)
    row_kernel = gauss_weights(out_index, in_index, float(height))
    illumination = jnp.einsum("hu,ucw->hcw", row_kernel, padded, precision=lax.Precision.HIGHEST)
    illum_round = (illumination * flat_gain.astype(jnp.float32)).astype(jnp.bfloat16)
    block = fields
    corrected = (
        block.astype(jnp.float32)
        / lax.all_gather(illum_round, "strip", axis=0, tiled=True).astype(jnp.float32)[None]
    ).astype(jnp.bfloat16)
    return (corrected, illumination, mean_field)


def solution(mesh):
    grid = mesh.shape["strip"] == 8 and mesh.shape["plate"] == 2
    return jax.shard_map(
        on_grid if grid else on_device,
        mesh=mesh,
        in_specs=(P(("batch", "strip", "plate"), None, None, None), P("strip", None, None)),
        out_specs=(
            P(("batch", "strip", "plate"), None, None, None),
            P("strip", "batch", None),
            P("strip", "batch", None),
        ),
        check_vma=False,
    )
```

```python
import jax
import jax.numpy as jnp
from jax import lax
from jax.experimental import pallas as pl
from jax.experimental.pallas import tpu as pltpu
from jax.sharding import PartitionSpec as P

SIGMA = 16
RADIUS = 48
ROWS = 8
WIDE = 256
COLUMNS = lax.Precision.HIGH
MESH = pl.DeviceIdType.MESH
LINK = jnp.bfloat16


def coded(mean):
    for _ in range(4):
        mean = mean * mean
    return mean.astype(LINK)


def decoded(code):
    code = code.astype(jnp.float32)
    for _ in range(4):
        code = lax.rsqrt(code)
    return code


def padded_2(array, sides, width):
    for axis, dim in sides:
        count, length = (lax.axis_size(axis), array.shape[dim])
        up = [(i, (i + 1) % count) for i in range(count - 1)]
        down = [(j, i) for i, j in up]
        last = lax.slice_in_dim(array, length - width, length, axis=dim)
        first = lax.slice_in_dim(array, 0, width, axis=dim)
        before = lax.ppermute(last, axis, up)
        after = lax.ppermute(first, axis, down)
        array = jnp.concatenate([before, array, after], axis=dim)
    return array


def gauss_weights(out_index, in_index, length):
    offset = out_index[:, None] - in_index[None, :]
    inside = (jnp.abs(offset) <= RADIUS) & (in_index[None, :] >= 0.0) & (in_index[None, :] < length)
    weights = jnp.where(inside, jnp.exp(-offset * offset / (2.0 * SIGMA * SIGMA)), 0.0)
    return weights / jnp.sum(weights, axis=1, keepdims=True)


def where_am_i():
    strip, plate = lax.axis_index("strip"), lax.axis_index("plate")
    return strip, plate, lax.rem(strip, 2), lax.div(strip, 2)


def at(strip, plate):
    return {"strip": strip, "plate": plate}


def greet(nz, strip, plate, y, z, halo=False):
    barrier = pltpu.get_barrier_semaphore()
    partners = [at(strip, 1 - plate), at(z * 2 + 1 - y, plate)]
    if halo:
        partners += [at(lax.rem(strip + d, nz * 2), 1 - plate) for d in (1, nz * 2 - 1)]
    partners += [at(lax.rem(z + d, nz) * 2 + y, plate) for d in range(1, nz)]
    for partner in partners:
        pl.semaphore_signal(barrier, inc=1, device_id=partner, device_id_type=MESH)
    pl.semaphore_wait(barrier, len(partners))


def reduce_kernel(x_ref, out_ref, raw, turned, sib, outbox, ybuf, zbuf, total,
                  load_sem, sib_send, sib_recv, y_send, y_recv, z_send, z_recv, t_send, t_recv, h_send, h_recv, o_sem):
    channels, nz, _, rows, width = turned.shape
    strip, plate, y, z = where_am_i()
    active = y == plate
    sibling = at(strip, 1 - plate)
    strips = nz * 2
    inner = pl.ds(RADIUS, rows)
    has_before, has_after = strip >= 1, strip + 1 < strips

    def load(c):
        return pltpu.make_async_copy(x_ref.at[c], raw.at[lax.rem(c, 2)], load_sem.at[c])

    def to_sibling(c):
        return pltpu.make_async_remote_copy(
            turned.at[c, :, 1 - plate], sib.at[c], sib_send.at[c], sib_recv.at[c],
            device_id=sibling, device_id_type=MESH)

    def across(c):
        return pltpu.make_async_remote_copy(
            outbox.at[c], ybuf.at[c], y_send.at[c], y_recv.at[c],
            device_id=at(z * 2 + 1 - y, plate), device_id_type=MESH)

    def along(c, d):
        return pltpu.make_async_remote_copy(
            outbox.at[c, d], zbuf.at[c, d], z_send.at[c, d], z_recv.at[c, d],
            device_id=at(lax.rem(z + d, nz) * 2 + y, plate), device_id_type=MESH)

    def halo_up(c):
        return pltpu.make_async_remote_copy(
            total.at[c, pl.ds(rows, RADIUS)], total.at[c, pl.ds(0, RADIUS)], h_send.at[c, 0], h_recv.at[c, 0],
            device_id=at(lax.rem(strip + 1, strips), 1 - plate), device_id_type=MESH)

    def halo_down(c):
        return pltpu.make_async_remote_copy(
            total.at[c, inner].at[pl.ds(0, RADIUS)], total.at[c, pl.ds(RADIUS + rows, RADIUS)],
            h_send.at[c, 1], h_recv.at[c, 1],
            device_id=at(lax.rem(strip + strips - 1, strips), 1 - plate), device_id_type=MESH)

    def share(c):
        return pltpu.make_async_remote_copy(
            total.at[c], total.at[c], t_send.at[c], t_recv.at[c],
            device_id=sibling, device_id_type=MESH)

    def store(c):
        return pltpu.make_async_copy(total.at[c], out_ref.at[c], o_sem.at[c])

    def turn(c):
        load(c).wait()
        for w in range(0, width, WIDE):
            wide = min(WIDE, width - w)
            block = jnp.transpose(raw[lax.rem(c, 2), pl.ds(w, wide), :])
            for k in range(nz * 2):
                turned[c, k // 2, k % 2, :, pl.ds(w, wide)] = block[k * rows:(k + 1) * rows]
        pl.when(c + 2 < channels)(lambda: load(c + 2).start())
        to_sibling(c).start()

    load(0).start()
    load(1).start()
    greet(nz, strip, plate, y, z, halo=True)
    turn(0)

    @pl.loop(0, channels)
    def _(c):
        pl.when(c + 1 < channels)(lambda: turn(c + 1))
        to_sibling(c).wait_recv()

        @pl.when(jnp.logical_not(active))
        def _():
            @pl.loop(0, nz)
            def _(k):
                for r in range(0, rows, ROWS):
                    at_r = pl.ds(r, ROWS)
                    value = turned[c, k, plate, at_r, :].astype(jnp.float32) + sib[c, k, at_r, :].astype(jnp.float32)
                    outbox[c, k, at_r, :] = coded(value * 0.5)

            across(c).start()

    @pl.when(active)
    def _():
        @pl.loop(0, channels)
        def _(c):
            across(c).wait_recv()

            def summed(k, r):
                at_r = pl.ds(r, ROWS)
                value = turned[c, k, plate, at_r, :].astype(jnp.float32) + sib[c, k, at_r, :].astype(jnp.float32)
                return value + 2.0 * decoded(ybuf[c, k, at_r, :])

            @pl.loop(1, nz)
            def _(d):
                k = lax.rem(z + d, nz)
                for r in range(0, rows, ROWS):
                    outbox[c, d, pl.ds(r, ROWS), :] = coded(summed(k, r) * 0.25)
                along(c, d).start()

            for r in range(0, rows, ROWS):
                total[c, pl.ds(RADIUS + r, ROWS), :] = summed(z, r)

        @pl.loop(0, channels)
        def _(c):
            @pl.loop(1, nz)
            def _(d):
                along(c, d).wait_recv()

            for r in range(0, rows, ROWS):
                at_r = pl.ds(r, ROWS)
                value = total[c, pl.ds(RADIUS + r, ROWS), :]
                for d in range(1, nz):
                    value = value + 4.0 * decoded(zbuf[c, d, at_r, :])
                total[c, pl.ds(RADIUS + r, ROWS), :] = value
            pl.when(has_after)(lambda: halo_up(c).start())
            pl.when(has_before)(lambda: halo_down(c).start())

        outside = jnp.zeros((RADIUS, width), jnp.float32)

        @pl.loop(0, channels)
        def _(c):
            @pl.when(has_before)
            def _():
                halo_up(c).wait_recv()

            @pl.when(jnp.logical_not(has_before))
            def _():
                total[c, pl.ds(0, RADIUS), :] = outside

            @pl.when(has_after)
            def _():
                halo_down(c).wait_recv()

            @pl.when(jnp.logical_not(has_after))
            def _():
                total[c, pl.ds(RADIUS + rows, RADIUS), :] = outside

            share(c).start()
            store(c).start()

        @pl.loop(0, channels)
        def _(c):
            share(c).wait_send()
            pl.when(has_after)(lambda: halo_up(c).wait_send())
            pl.when(has_before)(lambda: halo_down(c).wait_send())

            @pl.loop(1, nz)
            def _(d):
                along(c, d).wait_send()

    @pl.when(jnp.logical_not(active))
    def _():
        @pl.loop(0, channels)
        def _(c):
            share(c).wait_recv()
            store(c).start()
            across(c).wait_send()

    @pl.loop(0, channels)
    def _(c):
        to_sibling(c).wait_send()
        store(c).wait()


def strip_totals(x, nz):
    channels, width, height = x.shape
    rows = height // (nz * 2)
    part = (channels, nz, rows, width)
    dma = pltpu.SemaphoreType.DMA
    return pl.pallas_call(
        reduce_kernel,
        out_shape=jax.ShapeDtypeStruct((channels, rows + 2 * RADIUS, width), jnp.float32),
        in_specs=[pl.BlockSpec(memory_space=pl.ANY)],
        out_specs=pl.BlockSpec(memory_space=pl.ANY),
        scratch_shapes=[
            pltpu.VMEM((2, width, height), x.dtype), pltpu.VMEM((channels, nz, 2, rows, width), x.dtype),
            pltpu.VMEM(part, x.dtype), pltpu.VMEM(part, LINK), pltpu.VMEM(part, LINK), pltpu.VMEM(part, LINK),
            pltpu.VMEM((channels, rows + 2 * RADIUS, width), jnp.float32),
            dma((channels,)), dma((channels,)), dma((channels,)), dma((channels,)), dma((channels,)),
            dma((channels, nz)), dma((channels, nz)), dma((channels,)), dma((channels,)),
            dma((channels, 2)), dma((channels, 2)), dma((channels,)),
        ],
        compiler_params=pltpu.CompilerParams(
            collective_id=0, has_side_effects=True, vmem_limit_bytes=56 * 2**20),
        name="strip_totals",
    )(x)


def gather_kernel(own_ref, out_ref, own_sem, recv_sem, send_sem):
    channels, nz = out_ref.shape[:2]
    strip, plate, y, z = where_am_i()
    active = y == plate
    greet(nz, strip, plate, y, z)
    sibling, across = at(strip, 1 - plate), at(z * 2 + 1 - y, plate)
    above, below = at((z + 1) * 2 + y, plate), at((z - 1) * 2 + y, plate)

    def own(c):
        return pltpu.make_async_copy(own_ref.at[c], out_ref.at[c, z, y], own_sem.at[c])

    def send(c, k, column, kind, target, src=None):
        slot = out_ref.at[c, k, column]
        return pltpu.make_async_remote_copy(
            slot if src is None else src, slot, send_sem.at[c, k, kind], recv_sem.at[c, k, column],
            device_id=target, device_id_type=MESH)

    def sides(d, up, down):
        pl.when(z - d >= 0)(lambda: up(z - d))
        pl.when(z + d < nz)(lambda: down(z + d))

    @pl.when(active)
    def _():
        @pl.loop(0, channels)
        def _(c):
            own(c).start()
            pl.when(z + 1 < nz)(lambda: send(c, z, y, 2, above, own_ref.at[c]).start())
            pl.when(z >= 1)(lambda: send(c, z, y, 3, below, own_ref.at[c]).start())
            send(c, z, y, 1, across, own_ref.at[c]).start()
            send(c, z, y, 0, sibling, own_ref.at[c]).start()

        @pl.loop(1, nz)
        def _(d):
            @pl.loop(0, channels)
            def _(c):
                def up(k):
                    send(c, k, y, 2, above).wait_recv()
                    pl.when(z + 1 < nz)(lambda: send(c, k, y, 2, above).start())
                    send(c, k, y, 1, across).start()
                    send(c, k, y, 0, sibling).start()

                def down(k):
                    send(c, k, y, 3, below).wait_recv()
                    pl.when(z >= 1)(lambda: send(c, k, y, 3, below).start())
                    send(c, k, y, 1, across).start()
                    send(c, k, y, 0, sibling).start()

                sides(d, up, down)

        @pl.loop(0, channels)
        def _(c):
            own(c).wait()

            @pl.loop(0, nz)
            def _(k):
                send(c, k, 1 - y, 0, sibling).wait_recv()
                send(c, k, y, 0, sibling).wait_send()
                send(c, k, y, 1, across).wait_send()
                pl.when((k <= z) & (z + 1 < nz))(lambda: send(c, k, y, 2, above).wait_send())
                pl.when((k >= z) & (z >= 1))(lambda: send(c, k, y, 3, below).wait_send())

    @pl.when(jnp.logical_not(active))
    def _():
        @pl.loop(0, nz)
        def _(d):
            @pl.loop(0, channels)
            def _(c):
                def relay(k):
                    send(c, k, 1 - y, 0, sibling).wait_recv()
                    send(c, k, 1 - y, 0, sibling).start()

                pl.when(z - d >= 0)(lambda: relay(z - d))
                pl.when((z + d < nz) & (d > 0))(lambda: relay(z + d))

        @pl.loop(0, channels)
        def _(c):
            @pl.loop(0, nz)
            def _(k):
                send(c, k, y, 0, sibling).wait_recv()
                send(c, k, 1 - y, 0, sibling).wait_send()


def gathered(own, nz):
    channels, rows, width = own.shape
    dma = pltpu.SemaphoreType.DMA
    return pl.pallas_call(
        gather_kernel,
        out_shape=jax.ShapeDtypeStruct((channels, nz, 2, rows, width), own.dtype),
        in_specs=[pl.BlockSpec(memory_space=pl.ANY)],
        out_specs=pl.BlockSpec(memory_space=pl.ANY),
        scratch_shapes=[dma((channels,)), dma((channels, nz, 2)), dma((channels, nz, 4))],
        compiler_params=pltpu.CompilerParams(collective_id=1, has_side_effects=True),
        name="gathered",
    )(own)


def divide_kernel(field_ref, illum_ref, out_ref):
    illum = jnp.transpose(illum_ref[0]).astype(jnp.float32)
    out_ref[0] = (field_ref[0].astype(jnp.float32) / illum).astype(out_ref.dtype)


def divided(field, illum):
    channels, width, height = field.shape
    wide = WIDE
    upright = pl.BlockSpec((1, wide, height), lambda c, w: (c, w, 0))
    return pl.pallas_call(
        divide_kernel,
        grid=(channels, pl.cdiv(width, wide)),
        out_shape=jax.ShapeDtypeStruct(field.shape, field.dtype),
        in_specs=[upright, pl.BlockSpec((1, height, wide), lambda c, w: (c, 0, w))],
        out_specs=upright,
        compiler_params=pltpu.CompilerParams(vmem_limit_bytes=40 * 2**20),
        name="divided",
    )(field, illum)


def on_grid(fields, flat_gain):
    _, height, channels, width = fields.shape
    strips = lax.axis_size("strip")
    nz = strips // 2
    strip_rows = height // strips
    x = jnp.transpose(fields[0], (1, 2, 0))
    padded = strip_totals(x, nz) / (strips * 2)
    mean_field = padded[:, RADIUS:RADIUS + strip_rows]
    first_row = (lax.axis_index("strip") * strip_rows).astype(jnp.float32)
    out_index = first_row + jnp.arange(strip_rows, dtype=jnp.float32)
    in_index = first_row - RADIUS + jnp.arange(strip_rows + 2 * RADIUS, dtype=jnp.float32)
    row_kernel = gauss_weights(out_index, in_index, float(height))
    smooth_rows = jnp.einsum("hu,cuw->chw", row_kernel, padded, precision=lax.Precision.HIGHEST)
    col_index = jnp.arange(width, dtype=jnp.float32)
    col_kernel = gauss_weights(col_index, col_index, float(width))
    illumination = jnp.einsum("chv,wv->chw", smooth_rows, col_kernel, precision=COLUMNS)
    gain = jnp.transpose(flat_gain, (1, 0, 2)).astype(jnp.float32)
    illum_round = (illumination * gain).astype(jnp.bfloat16)
    everywhere = gathered(illum_round, nz).reshape(channels, height, width)
    corrected = divided(x, everywhere)
    back = lambda a: jnp.transpose(a, (1, 0, 2))
    return (jnp.transpose(corrected, (2, 0, 1))[None], back(illumination), back(mean_field))


def on_device(fields, flat_gain):
    num_fields, height, channels, width = fields.shape
    strips = lax.axis_size("strip")
    plates = lax.axis_size("plate")
    strip_rows = height // strips
    count = num_fields * strips * plates
    block = fields
    partial_sum = lax.psum_scatter(
        jnp.sum(block, axis=0, dtype=jnp.float32), "strip", scatter_dimension=0, tiled=True
    )
    total = lax.psum(partial_sum, "plate")
    mean_field = total / count
    col_index = jnp.arange(width, dtype=jnp.float32)
    col_kernel = gauss_weights(col_index, col_index, float(width))
    smooth_cols = jnp.einsum("hcv,wv->hcw", mean_field, col_kernel, precision=lax.Precision.HIGHEST)
    padded = padded_2(smooth_cols, (("strip", 0),), RADIUS)
    first_row = (lax.axis_index("strip") * strip_rows).astype(jnp.float32)
    out_index = first_row + jnp.arange(strip_rows, dtype=jnp.float32)
    in_index = first_row - RADIUS + jnp.arange(strip_rows + 2 * RADIUS, dtype=jnp.float32)
    row_kernel = gauss_weights(out_index, in_index, float(height))
    illumination = jnp.einsum("hu,ucw->hcw", row_kernel, padded, precision=lax.Precision.HIGHEST)
    illum_round = (illumination * flat_gain.astype(jnp.float32)).astype(jnp.bfloat16)
    block = fields
    corrected = (
        block.astype(jnp.float32)
        / lax.all_gather(illum_round, "strip", axis=0, tiled=True).astype(jnp.float32)[None]
    ).astype(jnp.bfloat16)
    return (corrected, illumination, mean_field)


def solution(mesh):
    grid = mesh.shape["strip"] == 8 and mesh.shape["plate"] == 2
    return jax.shard_map(
        on_grid if grid else on_device,
        mesh=mesh,
        in_specs=(P(("batch", "strip", "plate"), None, None, None), P("strip", None, None)),
        out_specs=(
            P(("batch", "strip", "plate"), None, None, None),
            P("strip", "batch", None),
            P("strip", "batch", None),
        ),
        check_vma=False,
    )
```

```python
import jax
import jax.numpy as jnp
from jax import lax
from jax.experimental import pallas as pl
from jax.experimental.pallas import tpu as pltpu
from jax.sharding import PartitionSpec as P

SIGMA = 16
RADIUS = 48
ROWS = 8
WIDE = 256
COLUMNS = lax.Precision.HIGH
MESH = pl.DeviceIdType.MESH
LINK = jnp.bfloat16


def coded(mean):
    for _ in range(4):
        mean = mean * mean
    return mean.astype(LINK)


def decoded(code):
    code = code.astype(jnp.float32)
    for _ in range(4):
        code = lax.rsqrt(code)
    return code


def padded_2(array, sides, width):
    for axis, dim in sides:
        count, length = (lax.axis_size(axis), array.shape[dim])
        up = [(i, (i + 1) % count) for i in range(count - 1)]
        down = [(j, i) for i, j in up]
        last = lax.slice_in_dim(array, length - width, length, axis=dim)
        first = lax.slice_in_dim(array, 0, width, axis=dim)
        before = lax.ppermute(last, axis, up)
        after = lax.ppermute(first, axis, down)
        array = jnp.concatenate([before, array, after], axis=dim)
    return array


def gauss_weights(out_index, in_index, length):
    offset = out_index[:, None] - in_index[None, :]
    inside = (jnp.abs(offset) <= RADIUS) & (in_index[None, :] >= 0.0) & (in_index[None, :] < length)
    weights = jnp.where(inside, jnp.exp(-offset * offset / (2.0 * SIGMA * SIGMA)), 0.0)
    return weights / jnp.sum(weights, axis=1, keepdims=True)


def where_am_i():
    strip, plate = lax.axis_index("strip"), lax.axis_index("plate")
    return strip, plate, lax.rem(strip, 2), lax.div(strip, 2)


def at(strip, plate):
    return {"strip": strip, "plate": plate}


def greet(nz, strip, plate, y, z, halo=False):
    barrier = pltpu.get_barrier_semaphore()
    partners = [at(strip, 1 - plate), at(z * 2 + 1 - y, plate)]
    if halo:
        partners += [at(lax.rem(strip + d, nz * 2), 1 - plate) for d in (1, nz * 2 - 1)]
    partners += [at(lax.rem(z + d, nz) * 2 + y, plate) for d in range(1, nz)]
    for partner in partners:
        pl.semaphore_signal(barrier, inc=1, device_id=partner, device_id_type=MESH)
    pl.semaphore_wait(barrier, len(partners))


def reduce_kernel(x_ref, out_ref, raw, turned, sib, outbox, ybuf, zbuf, total,
                  load_sem, sib_send, sib_recv, y_send, y_recv, z_send, z_recv, t_send, t_recv, h_send, h_recv, o_sem):
    channels, nz, _, rows, width = turned.shape
    strip, plate, y, z = where_am_i()
    active = y == plate
    sibling = at(strip, 1 - plate)
    strips = nz * 2
    inner = pl.ds(RADIUS, rows)
    has_before, has_after = strip >= 1, strip + 1 < strips

    def load(c):
        return pltpu.make_async_copy(x_ref.at[c], raw.at[lax.rem(c, 2)], load_sem.at[c])

    def to_sibling(c):
        return pltpu.make_async_remote_copy(
            turned.at[c, :, 1 - plate], sib.at[c], sib_send.at[c], sib_recv.at[c],
            device_id=sibling, device_id_type=MESH)

    def across(c):
        return pltpu.make_async_remote_copy(
            outbox.at[c], ybuf.at[c], y_send.at[c], y_recv.at[c],
            device_id=at(z * 2 + 1 - y, plate), device_id_type=MESH)

    def along(c, d):
        return pltpu.make_async_remote_copy(
            outbox.at[c, d], zbuf.at[c, d], z_send.at[c, d], z_recv.at[c, d],
            device_id=at(lax.rem(z + d, nz) * 2 + y, plate), device_id_type=MESH)

    def halo_up(c):
        return pltpu.make_async_remote_copy(
            total.at[c, pl.ds(rows, RADIUS)], total.at[c, pl.ds(0, RADIUS)], h_send.at[c, 0], h_recv.at[c, 0],
            device_id=at(lax.rem(strip + 1, strips), 1 - plate), device_id_type=MESH)

    def halo_down(c):
        return pltpu.make_async_remote_copy(
            total.at[c, inner].at[pl.ds(0, RADIUS)], total.at[c, pl.ds(RADIUS + rows, RADIUS)],
            h_send.at[c, 1], h_recv.at[c, 1],
            device_id=at(lax.rem(strip + strips - 1, strips), 1 - plate), device_id_type=MESH)

    def share(c):
        return pltpu.make_async_remote_copy(
            total.at[c], total.at[c], t_send.at[c], t_recv.at[c],
            device_id=sibling, device_id_type=MESH)

    def store(c):
        return pltpu.make_async_copy(total.at[c], out_ref.at[c], o_sem.at[c])

    def turn(c):
        load(c).wait()
        for w in range(0, width, WIDE):
            wide = min(WIDE, width - w)
            block = jnp.transpose(raw[lax.rem(c, 2), pl.ds(w, wide), :])
            for k in range(nz * 2):
                turned[c, k // 2, k % 2, :, pl.ds(w, wide)] = block[k * rows:(k + 1) * rows]
        pl.when(c + 2 < channels)(lambda: load(c + 2).start())
        to_sibling(c).start()

    load(0).start()
    load(1).start()
    greet(nz, strip, plate, y, z, halo=True)
    turn(0)

    @pl.loop(0, channels)
    def _(c):
        pl.when(c + 1 < channels)(lambda: turn(c + 1))
        to_sibling(c).wait_recv()

        @pl.when(jnp.logical_not(active))
        def _():
            @pl.loop(0, nz)
            def _(k):
                for r in range(0, rows, ROWS):
                    at_r = pl.ds(r, ROWS)
                    value = turned[c, k, plate, at_r, :].astype(jnp.float32) + sib[c, k, at_r, :].astype(jnp.float32)
                    outbox[c, k, at_r, :] = coded(value * 0.5)

            across(c).start()

    @pl.when(active)
    def _():
        @pl.loop(0, channels)
        def _(c):
            across(c).wait_recv()

            def summed(k, r):
                at_r = pl.ds(r, ROWS)
                value = turned[c, k, plate, at_r, :].astype(jnp.float32) + sib[c, k, at_r, :].astype(jnp.float32)
                return value + 2.0 * decoded(ybuf[c, k, at_r, :])

            @pl.loop(1, nz)
            def _(d):
                k = lax.rem(z + d, nz)
                for r in range(0, rows, ROWS):
                    outbox[c, d, pl.ds(r, ROWS), :] = coded(summed(k, r) * 0.25)
                along(c, d).start()

            for r in range(0, rows, ROWS):
                total[c, pl.ds(RADIUS + r, ROWS), :] = summed(z, r)

        @pl.loop(0, channels)
        def _(c):
            @pl.loop(1, nz)
            def _(d):
                along(c, d).wait_recv()

            for r in range(0, rows, ROWS):
                at_r = pl.ds(r, ROWS)
                value = total[c, pl.ds(RADIUS + r, ROWS), :]
                for d in range(1, nz):
                    value = value + 4.0 * decoded(zbuf[c, d, at_r, :])
                total[c, pl.ds(RADIUS + r, ROWS), :] = value
            pl.when(has_after)(lambda: halo_up(c).start())
            pl.when(has_before)(lambda: halo_down(c).start())

        outside = jnp.zeros((RADIUS, width), jnp.float32)

        @pl.loop(0, channels)
        def _(c):
            @pl.when(has_before)
            def _():
                halo_up(c).wait_recv()

            @pl.when(jnp.logical_not(has_before))
            def _():
                total[c, pl.ds(0, RADIUS), :] = outside

            @pl.when(has_after)
            def _():
                halo_down(c).wait_recv()

            @pl.when(jnp.logical_not(has_after))
            def _():
                total[c, pl.ds(RADIUS + rows, RADIUS), :] = outside

            share(c).start()
            store(c).start()

        @pl.loop(0, channels)
        def _(c):
            share(c).wait_send()
            pl.when(has_after)(lambda: halo_up(c).wait_send())
            pl.when(has_before)(lambda: halo_down(c).wait_send())

            @pl.loop(1, nz)
            def _(d):
                along(c, d).wait_send()

    @pl.when(jnp.logical_not(active))
    def _():
        @pl.loop(0, channels)
        def _(c):
            share(c).wait_recv()
            store(c).start()
            across(c).wait_send()

    @pl.loop(0, channels)
    def _(c):
        to_sibling(c).wait_send()
        store(c).wait()


def strip_totals(x, nz):
    channels, width, height = x.shape
    rows = height // (nz * 2)
    part = (channels, nz, rows, width)
    dma = pltpu.SemaphoreType.DMA
    return pl.pallas_call(
        reduce_kernel,
        out_shape=jax.ShapeDtypeStruct((channels, rows + 2 * RADIUS, width), jnp.float32),
        in_specs=[pl.BlockSpec(memory_space=pl.ANY)],
        out_specs=pl.BlockSpec(memory_space=pl.ANY),
        scratch_shapes=[
            pltpu.VMEM((2, width, height), x.dtype), pltpu.VMEM((channels, nz, 2, rows, width), x.dtype),
            pltpu.VMEM(part, x.dtype), pltpu.VMEM(part, LINK), pltpu.VMEM(part, LINK), pltpu.VMEM(part, LINK),
            pltpu.VMEM((channels, rows + 2 * RADIUS, width), jnp.float32),
            dma((channels,)), dma((channels,)), dma((channels,)), dma((channels,)), dma((channels,)),
            dma((channels, nz)), dma((channels, nz)), dma((channels,)), dma((channels,)),
            dma((channels, 2)), dma((channels, 2)), dma((channels,)),
        ],
        compiler_params=pltpu.CompilerParams(
            collective_id=0, has_side_effects=True, vmem_limit_bytes=56 * 2**20),
        name="strip_totals",
    )(x)


def gather_kernel(own_ref, out_ref, own_sem, recv_sem, send_sem):
    channels, nz = out_ref.shape[:2]
    strip, plate, y, z = where_am_i()
    active = y == plate
    greet(nz, strip, plate, y, z)
    sibling, across = at(strip, 1 - plate), at(z * 2 + 1 - y, plate)
    above, below = at((z + 1) * 2 + y, plate), at((z - 1) * 2 + y, plate)

    def own(c):
        return pltpu.make_async_copy(own_ref.at[c], out_ref.at[c, z, y], own_sem.at[c])

    def send(c, k, column, kind, target, src=None):
        slot = out_ref.at[c, k, column]
        return pltpu.make_async_remote_copy(
            slot if src is None else src, slot, send_sem.at[c, k, kind], recv_sem.at[c, k, column],
            device_id=target, device_id_type=MESH)

    def sides(d, up, down):
        pl.when(z - d >= 0)(lambda: up(z - d))
        pl.when(z + d < nz)(lambda: down(z + d))

    @pl.when(active)
    def _():
        @pl.loop(0, channels)
        def _(c):
            own(c).start()
            pl.when(z + 1 < nz)(lambda: send(c, z, y, 2, above, own_ref.at[c]).start())
            pl.when(z >= 1)(lambda: send(c, z, y, 3, below, own_ref.at[c]).start())
            send(c, z, y, 1, across, own_ref.at[c]).start()
            send(c, z, y, 0, sibling, own_ref.at[c]).start()

        @pl.loop(1, nz)
        def _(d):
            @pl.loop(0, channels)
            def _(c):
                def up(k):
                    send(c, k, y, 2, above).wait_recv()
                    pl.when(z + 1 < nz)(lambda: send(c, k, y, 2, above).start())
                    send(c, k, y, 1, across).start()
                    send(c, k, y, 0, sibling).start()

                def down(k):
                    send(c, k, y, 3, below).wait_recv()
                    pl.when(z >= 1)(lambda: send(c, k, y, 3, below).start())
                    send(c, k, y, 1, across).start()
                    send(c, k, y, 0, sibling).start()

                sides(d, up, down)

        @pl.loop(0, channels)
        def _(c):
            own(c).wait()

            @pl.loop(0, nz)
            def _(k):
                send(c, k, 1 - y, 0, sibling).wait_recv()
                send(c, k, y, 0, sibling).wait_send()
                send(c, k, y, 1, across).wait_send()
                pl.when((k <= z) & (z + 1 < nz))(lambda: send(c, k, y, 2, above).wait_send())
                pl.when((k >= z) & (z >= 1))(lambda: send(c, k, y, 3, below).wait_send())

    @pl.when(jnp.logical_not(active))
    def _():
        @pl.loop(0, nz)
        def _(d):
            @pl.loop(0, channels)
            def _(c):
                def relay(k):
                    send(c, k, 1 - y, 0, sibling).wait_recv()
                    send(c, k, 1 - y, 0, sibling).start()

                pl.when(z - d >= 0)(lambda: relay(z - d))
                pl.when((z + d < nz) & (d > 0))(lambda: relay(z + d))

        @pl.loop(0, channels)
        def _(c):
            @pl.loop(0, nz)
            def _(k):
                send(c, k, y, 0, sibling).wait_recv()
                send(c, k, 1 - y, 0, sibling).wait_send()


def gathered(own, nz):
    channels, rows, width = own.shape
    dma = pltpu.SemaphoreType.DMA
    return pl.pallas_call(
        gather_kernel,
        out_shape=jax.ShapeDtypeStruct((channels, nz, 2, rows, width), own.dtype),
        in_specs=[pl.BlockSpec(memory_space=pl.ANY)],
        out_specs=pl.BlockSpec(memory_space=pl.ANY),
        scratch_shapes=[dma((channels,)), dma((channels, nz, 2)), dma((channels, nz, 4))],
        compiler_params=pltpu.CompilerParams(collective_id=1, has_side_effects=True),
        name="gathered",
    )(own)


def divide_kernel(field_ref, illum_ref, out_ref):
    illum = jnp.transpose(illum_ref[0]).astype(jnp.float32)
    out_ref[0] = (field_ref[0].astype(jnp.float32) / illum).astype(out_ref.dtype)


def divided(field, illum):
    channels, width, height = field.shape
    wide = 384
    upright = pl.BlockSpec((1, wide, height), lambda c, w: (c, w, 0))
    return pl.pallas_call(
        divide_kernel,
        grid=(channels, pl.cdiv(width, wide)),
        out_shape=jax.ShapeDtypeStruct(field.shape, field.dtype),
        in_specs=[upright, pl.BlockSpec((1, height, wide), lambda c, w: (c, 0, w))],
        out_specs=upright,
        compiler_params=pltpu.CompilerParams(vmem_limit_bytes=40 * 2**20),
        name="divided",
    )(field, illum)


def on_grid(fields, flat_gain):
    _, height, channels, width = fields.shape
    strips = lax.axis_size("strip")
    nz = strips // 2
    strip_rows = height // strips
    x = jnp.transpose(fields[0], (1, 2, 0))
    padded = strip_totals(x, nz) / (strips * 2)
    mean_field = padded[:, RADIUS:RADIUS + strip_rows]
    first_row = (lax.axis_index("strip") * strip_rows).astype(jnp.float32)
    out_index = first_row + jnp.arange(strip_rows, dtype=jnp.float32)
    in_index = first_row - RADIUS + jnp.arange(strip_rows + 2 * RADIUS, dtype=jnp.float32)
    row_kernel = gauss_weights(out_index, in_index, float(height))
    smooth_rows = jnp.einsum("hu,cuw->chw", row_kernel, padded, precision=lax.Precision.HIGHEST)
    col_index = jnp.arange(width, dtype=jnp.float32)
    col_kernel = gauss_weights(col_index, col_index, float(width))
    illumination = jnp.einsum("chv,wv->chw", smooth_rows, col_kernel, precision=COLUMNS)
    gain = jnp.transpose(flat_gain, (1, 0, 2)).astype(jnp.float32)
    illum_round = (illumination * gain).astype(jnp.bfloat16)
    everywhere = gathered(illum_round, nz).reshape(channels, height, width)
    corrected = divided(x, everywhere)
    back = lambda a: jnp.transpose(a, (1, 0, 2))
    return (jnp.transpose(corrected, (2, 0, 1))[None], back(illumination), back(mean_field))


def on_device(fields, flat_gain):
    num_fields, height, channels, width = fields.shape
    strips = lax.axis_size("strip")
    plates = lax.axis_size("plate")
    strip_rows = height // strips
    count = num_fields * strips * plates
    block = fields
    partial_sum = lax.psum_scatter(
        jnp.sum(block, axis=0, dtype=jnp.float32), "strip", scatter_dimension=0, tiled=True
    )
    total = lax.psum(partial_sum, "plate")
    mean_field = total / count
    col_index = jnp.arange(width, dtype=jnp.float32)
    col_kernel = gauss_weights(col_index, col_index, float(width))
    smooth_cols = jnp.einsum("hcv,wv->hcw", mean_field, col_kernel, precision=lax.Precision.HIGHEST)
    padded = padded_2(smooth_cols, (("strip", 0),), RADIUS)
    first_row = (lax.axis_index("strip") * strip_rows).astype(jnp.float32)
    out_index = first_row + jnp.arange(strip_rows, dtype=jnp.float32)
    in_index = first_row - RADIUS + jnp.arange(strip_rows + 2 * RADIUS, dtype=jnp.float32)
    row_kernel = gauss_weights(out_index, in_index, float(height))
    illumination = jnp.einsum("hu,ucw->hcw", row_kernel, padded, precision=lax.Precision.HIGHEST)
    illum_round = (illumination * flat_gain.astype(jnp.float32)).astype(jnp.bfloat16)
    block = fields
    corrected = (
        block.astype(jnp.float32)
        / lax.all_gather(illum_round, "strip", axis=0, tiled=True).astype(jnp.float32)[None]
    ).astype(jnp.bfloat16)
    return (corrected, illumination, mean_field)


def solution(mesh):
    grid = mesh.shape["strip"] == 8 and mesh.shape["plate"] == 2
    return jax.shard_map(
        on_grid if grid else on_device,
        mesh=mesh,
        in_specs=(P(("batch", "strip", "plate"), None, None, None), P("strip", None, None)),
        out_specs=(
            P(("batch", "strip", "plate"), None, None, None),
            P("strip", "batch", None),
            P("strip", "batch", None),
        ),
        check_vma=False,
    )
```
